32 devices in a mesh: groups: 2 (over y), patch: 8 (over z, x), batch: 2 (over core).
Axes of the slice: x: 2, y: 2, z: 4, core: 2. Of those that a mesh axis runs over, the one named last changes fastest.
Arguments:
- subjects: bfloat16 [2048, 3, 20480], P(('groups', 'batch'), None, 'patch'), parts along dimension 0, may hold values from -6 to 6
- basis_modes: bfloat16 [3, 40960, 128], P(None, ('groups', 'patch')), parts along dimension 1, may hold values from -21 to 21
- laplace_blocks: bfloat16 [320, 4, 64, 64], P('patch'), may hold values from -0.29882812 to 0.29882812
- columns: int32 [320, 4], P('patch'), may hold values from 0 to 319, as said below
Outputs:
- scores: float32 [2048, 128], P(('groups', 'batch')), parts along dimension 0
- new_modes: bfloat16 [3, 40960, 128], P(None, ('groups', 'patch')), parts along dimension 1
- mode_norms: float32 [256], P('groups'), parts along dimension 0
The draws below stay inside these ranges and needn't reach their ends.
There are 2 independent parts, one for each index of `groups`. The reference program is written for one: setup_inputs(seed, part) draws one part's arguments, and reference() takes and returns one part's arrays. A program takes and returns all parts, laid end to end along the dimension named above; an argument that names none is the same for every part. Nothing has to cross between parts.
Inputs may be any that keep to these rules, and one draw needn't show every extreme that they name: columns[i, 0] = i; with 40 blocks a patch, an entry of block row i lies in i's own patch, except that in the last 4 block rows of a patch an entry may also lie among the first 4 blocks of the next patch; entries of a row may repeat.
All inputs are finite; a program needn't handle non-finite values.
Results may differ from the reference program's by a relative error of at most 0.0034.
Values may be sent and summed in bfloat16 or wider, within the bound.
A program may use at most 192 MiB of HBM per device.

```python
import math
import jax
import jax.numpy as jnp
from jax import lax

K = 128
VERT_DEV = 2560
NB = 4
GHOST = 4
BLK_DEV = 40
VERTS = 20480
BLOCKS = 320
COORDS = 61440
BATCH = 1024
N_PATCH = 8


def draw_columns(key, part):
    rows_id = jnp.arange(BLOCKS, dtype=jnp.int32)
    patch_of = rows_id // BLK_DEV
    local_row = rows_id % BLK_DEV
    last_patch = BLOCKS // BLK_DEV - 1
    raw_cols = jax.random.randint(key, (BLOCKS, NB), 0, 2 * BLK_DEV * GHOST, dtype=jnp.int32)
    interior = patch_of[:, None] * BLK_DEV + raw_cols % BLK_DEV
    folded = raw_cols % (2 * GHOST)
    edge_own = patch_of[:, None] * BLK_DEV + BLK_DEV - GHOST + folded % GHOST
    edge_next = (patch_of[:, None] + 1) * BLK_DEV + folded - GHOST
    reach_next = (folded >= GHOST) & (patch_of[:, None] != last_patch)
    edge_pick = jnp.where(reach_next, edge_next, edge_own)
    is_edge = (local_row >= BLK_DEV - GHOST)[:, None]
    picked = jnp.where(is_edge, edge_pick, interior)
    slot_id = jnp.arange(NB, dtype=jnp.int32)[None, :]
    return jnp.where(slot_id == 0, rows_id[:, None], picked).astype(jnp.int32)


def draw_basis_modes(key, part):
    key_base, key_rough, key_col = jax.random.split(key, 3)
    position = jnp.arange(VERTS, dtype=jnp.float32) / VERTS
    ramp = jnp.sqrt((1.0 + 9.0 * position) / 5.5)
    rough = jnp.exp(jax.random.uniform(key_rough, (3, VERTS, 1), jnp.float32, -0.4, 0.4))
    base = jnp.clip(jax.random.normal(key_base, (3, VERTS, K), jnp.float32), -4.0, 4.0)
    col_scale = jnp.exp(jax.random.uniform(key_col, (K,), jnp.float32, math.log(0.25), math.log(2.5)))
    return (base * ramp[None, :, None] * rough * col_scale[None, None, :]).astype(jnp.bfloat16)


def steps_of(rng, extent, shards, least, largest):
    loudness, own = 1.0, jax.random.fold_in(rng, 6)
    for dim, shards_of in shards:
        heights = jnp.exp(jax.random.uniform(jax.random.fold_in(own, dim), (shards_of,), jnp.float32, least / len(shards), largest / len(shards)))
        loudness = loudness * jnp.repeat(heights, extent[dim] // shards_of).reshape([-1 if axis == dim else 1 for axis in range(len(extent))])
    return loudness


def gaussian(own_key, extent, scale, reach, pieces=(), kind=jnp.bfloat16):
    gain = steps_of(own_key, extent, pieces, -0.22, 0.18) if pieces else 1.0
    result = jax.random.normal(own_key, extent, jnp.float32) * scale * gain
    return jnp.minimum(jnp.maximum(result, -reach), reach).astype(kind)


def setup_inputs(seed: int = 0, part: int = 0) -> dict:
    seeds = jax.random.split(jax.random.key(seed), 5)
    part_splits = jax.random.split(jax.random.fold_in(seeds[4], part), 5)
    subjects = gaussian(part_splits[0], (BATCH, 3, VERTS), 1.0, 6.0, ((0, 2), (2, 8)))
    basis_modes = draw_basis_modes(jax.random.fold_in(jax.random.fold_in(seeds[4], part), 71), part)
    laplace_blocks = gaussian(seeds[2], (BLOCKS, NB, 64, 64), 0.05, 0.29882812, ((0, 8),))
    columns = draw_columns(jax.random.fold_in(seeds[4], 71), part)
    return {"subjects": subjects, "basis_modes": basis_modes, "laplace_blocks": laplace_blocks, "columns": columns}


HIGH = lax.Precision.HIGHEST

def reference(subjects, basis_modes, laplace_blocks, columns):
    scale_inv = 1.0 / math.sqrt(COORDS)
    blocks_f = laplace_blocks.astype(jnp.float32)
    weights = basis_modes.astype(jnp.float32)
    grid = weights.reshape(3, BLOCKS, 64, K)
    flat_cols = columns.reshape(-1)
    degree = blocks_f.sum(axis=(1, 3)) + jax.ops.segment_sum(blocks_f.sum(axis=2).reshape(BLOCKS * NB, 64), flat_cols, num_segments=BLOCKS)
    smooth = degree[None, :, :, None] * grid
    for column in range(NB):
        block_n = blocks_f[:, column]
        picked = jnp.take(grid, columns[:, column], axis=1)
        smooth = smooth - jnp.einsum('bij,cbjk->cbik', block_n, picked, precision=HIGH)
        moved = jnp.einsum('bij,cbik->bcjk', block_n, grid, precision=HIGH)
        smooth = smooth - jax.ops.segment_sum(moved, columns[:, column], num_segments=BLOCKS).transpose(1, 0, 2, 3)
    smooth = smooth.reshape(3, VERTS, K)

    def score_step(patch_id, carry):
        offset = (patch_id * VERT_DEV).astype(jnp.int32)
        piece = lax.dynamic_slice_in_dim(subjects, offset, VERT_DEV, 2).astype(jnp.float32)
        wpiece = lax.dynamic_slice_in_dim(weights, offset, VERT_DEV, 1)
        return carry + jnp.einsum('bcv,cvk->bk', piece, wpiece, precision=HIGH)
    scores = lax.fori_loop(0, N_PATCH, score_step, jnp.zeros((BATCH, K), jnp.float32)) * scale_inv
    low = lax.optimization_barrier(scores.astype(jnp.bfloat16)).astype(jnp.float32)

    def update_piece(patch_id):
        offset = (patch_id * VERT_DEV).astype(jnp.int32)
        piece = lax.dynamic_slice_in_dim(subjects, offset, VERT_DEV, 2).astype(jnp.float32)
        wpiece = lax.dynamic_slice_in_dim(weights, offset, VERT_DEV, 1)
        spiece = lax.dynamic_slice_in_dim(smooth, offset, VERT_DEV, 1)
        recon = jnp.einsum('bk,cvk->bcv', low, wpiece, precision=HIGH) * scale_inv
        resid = lax.optimization_barrier((piece - recon).astype(jnp.bfloat16)).astype(jnp.float32)
        hebb = jnp.einsum('bcv,bk->cvk', resid, low, precision=HIGH)
        return wpiece + 4.0 / BATCH * hebb - 0.2 * spiece
    updated = lax.map(update_piece, jnp.arange(N_PATCH, dtype=jnp.int32))
    updated = updated.transpose(1, 0, 2, 3).reshape(3, VERTS, K)
    norms = jnp.sqrt(lax.optimization_barrier(jnp.mean(updated * updated, axis=(0, 1))) + 1e-06)
    return (scores, (updated / norms).astype(jnp.bfloat16), norms)
```

```python
import functools
import math

import jax
import jax.numpy as jnp
from jax import lax
from jax.experimental import pallas as pl
from jax.experimental.pallas import tpu as pltpu
from jax.sharding import PartitionSpec as P

GHOST = 4
MESH = pl.DeviceIdType.MESH
VMEM = pl.BlockSpec(memory_space=pltpu.VMEM)
SMEM = pl.BlockSpec(memory_space=pltpu.SMEM)
LIMIT = 60 * 1024 * 1024


def shifted(value, axis, steps):
    count = lax.axis_size(axis)
    initial, last = (max(0, -steps), min(count, count - steps))
    return lax.ppermute(value, axis, [(source, source + steps) for source in range(initial, last)])


def greet(n, axis):
    me = lax.axis_index(axis)
    barrier = pltpu.get_barrier_semaphore()
    for step in range(1, n):
        pl.semaphore_signal(
            barrier, inc=1, device_id={axis: lax.rem(me + step, n)}, device_id_type=MESH
        )
    pl.semaphore_wait(barrier, n - 1)
    return me


def sum_kernel(n, scale, part_ref, out_ref, low_ref, land, full, send_a, recv_a, send_b, recv_b):
    me = greet(n, "patch")
    rows = part_ref.shape[0] // n
    copies = []
    for step in range(1, n):
        to = lax.rem(me + step, n)
        copy = pltpu.make_async_remote_copy(
            src_ref=part_ref.at[pl.ds(pl.multiple_of(to * rows, rows), rows)],
            dst_ref=land.at[step],
            send_sem=send_a.at[step],
            recv_sem=recv_a.at[step],
            device_id={"patch": to},
            device_id_type=MESH,
        )
        copy.start()
        copies.append(copy)
    own = pl.ds(pl.multiple_of(me * rows, rows), rows)
    total = part_ref[own, :]
    for step, copy in enumerate(copies, 1):
        copy.wait()
        total = total + land[step]
    full[own, :] = total * scale
    copies = []
    for step in range(1, n):
        to = lax.rem(me + step, n)
        copy = pltpu.make_async_remote_copy(
            src_ref=full.at[own],
            dst_ref=full.at[own],
            send_sem=send_b.at[step],
            recv_sem=recv_b.at[step],
            device_id={"patch": to},
            device_id_type=MESH,
        )
        copy.start()
        copies.append(copy)
    for copy in copies:
        copy.wait()
    out_ref[...] = full[...]
    low_ref[...] = full[...].astype(jnp.bfloat16)


def reduce_scores(partial_value, scale):
    n = lax.axis_size("patch")
    rows, width = partial_value.shape
    return pl.pallas_call(
        functools.partial(sum_kernel, n, scale),
        out_shape=(
            jax.ShapeDtypeStruct((rows, width), jnp.float32),
            jax.ShapeDtypeStruct((rows, width), jnp.bfloat16),
        ),
        in_specs=[VMEM],
        out_specs=(VMEM, VMEM),
        scratch_shapes=[
            pltpu.VMEM((n, rows // n, width), jnp.float32),
            pltpu.VMEM((rows, width), jnp.float32),
        ]
        + [pltpu.SemaphoreType.DMA((n,))] * 4,
        compiler_params=pltpu.CompilerParams(collective_id=0, has_side_effects=True),
        name="reduce_scores",
    )(partial_value)


def smooth_kernel(cols, back_cols, blocks, back_blocks, modes, after, before, out, wide, acc):
    count, per_row, side, _ = blocks.shape
    coords, verts, width = modes.shape
    reach = after.shape[1]
    ones = jnp.ones((wide.shape[0], width), jnp.bfloat16)
    for c in range(coords):
        lanes = slice(c * width, (c + 1) * width)
        wide[:verts, lanes] = modes[c]
        wide[verts : verts + reach, lanes] = after[c]
        wide[verts + reach :, lanes] = before[c]
    wide[:, coords * width :] = ones
    acc[...] = jnp.zeros_like(acc)

    def rows_of(block):
        return pl.ds(pl.multiple_of(block * side, side), side)

    def scatter(joined, block, targets):
        moved = lax.dot_general(
            joined,
            wide[rows_of(block), :],
            (((0,), (0,)), ((), ())),
            preferred_element_type=jnp.float32,
        )
        for slot, target in enumerate(targets):
            acc[rows_of(target), :] += moved[slot * side : (slot + 1) * side]

    def step(i, _):
        joined = jnp.concatenate([blocks[i, slot] for slot in range(per_row)], axis=1)
        targets = [cols[i, slot] for slot in range(per_row)]
        picked = jnp.concatenate([wide[rows_of(t), :] for t in targets], axis=0)
        acc[rows_of(i), :] += jnp.dot(joined, picked, preferred_element_type=jnp.float32)
        scatter(joined, i, targets)
        return 0

    lax.fori_loop(0, count, step, 0)

    def back_step(i, _):
        joined = jnp.concatenate([back_blocks[i, slot] for slot in range(per_row)], axis=1)
        targets = [back_cols[i, slot] for slot in range(per_row)]
        scatter(joined, count + reach // side + i, targets)
        return 0

    lax.fori_loop(0, back_blocks.shape[0], back_step, 0)

    def finish(i, _):
        rows = rows_of(i)
        degree = acc[rows, coords * width :]
        for c in range(coords):
            mode = modes[c, rows, :].astype(jnp.float32)
            out[c, rows, :] = mode - 0.2 * (
                degree * mode - acc[rows, c * width : (c + 1) * width]
            )
        return 0

    lax.fori_loop(0, count, finish, 0)


def smoothed(basis_modes, laplace_blocks, columns):
    count, per_row, side, _ = laplace_blocks.shape
    coords, verts, width = basis_modes.shape
    reach = GHOST * side
    first = lax.axis_index("patch") * count
    after = shifted(basis_modes[:, :reach], "patch", -1)
    before = shifted(basis_modes[:, verts - reach :], "patch", 1)
    back_blocks = shifted(laplace_blocks[count - GHOST :], "patch", 1)
    back_cols = shifted(columns[count - GHOST :], "patch", 1)
    total = count + 2 * GHOST
    cols = columns - first
    back = back_cols - first
    back = jnp.where((back >= 0) & (back < GHOST), back, total - 1)
    return pl.pallas_call(
        smooth_kernel,
        out_shape=jax.ShapeDtypeStruct((coords, verts, width), jnp.float32),
        in_specs=[SMEM, SMEM] + [VMEM] * 5,
        out_specs=VMEM,
        scratch_shapes=[
            pltpu.VMEM((total * side, (coords + 1) * width), jnp.bfloat16),
            pltpu.VMEM((total * side, (coords + 1) * width), jnp.float32),
        ],
        compiler_params=pltpu.CompilerParams(vmem_limit_bytes=LIMIT),
        name="smooth",
    )(cols, back, laplace_blocks, back_blocks, basis_modes, after, before)


def hebb_kernel(scale, x_ref, low_ref, turned_ref, mode_ref, out_ref):
    recon = lax.dot_general(
        low_ref[...], mode_ref[0], (((1,), (1,)), ((), ())), preferred_element_type=jnp.float32
    )
    residual = (x_ref[0].astype(jnp.float32) - recon * scale).astype(jnp.bfloat16)
    hebb = jnp.dot(turned_ref[...], residual, preferred_element_type=jnp.float32)
    out_ref[0] = hebb.T.astype(jnp.bfloat16)


def hebbian(planes, low, basis_modes, scale):
    coords, subjects, verts = planes.shape
    width = basis_modes.shape[2]
    tile = math.gcd(verts, 512)
    return pl.pallas_call(
        functools.partial(hebb_kernel, scale),
        out_shape=jax.ShapeDtypeStruct((coords, verts, width), jnp.bfloat16),
        grid=(coords, verts // tile),
        in_specs=[
            pl.BlockSpec((1, subjects, tile), lambda c, v: (c, 0, v)),
            pl.BlockSpec((subjects, width), lambda c, v: (0, 0)),
            pl.BlockSpec((width, subjects), lambda c, v: (0, 0)),
            pl.BlockSpec((1, tile, width), lambda c, v: (c, v, 0)),
        ],
        out_specs=pl.BlockSpec((1, tile, width), lambda c, v: (c, v, 0)),
        compiler_params=pltpu.CompilerParams(vmem_limit_bytes=LIMIT),
        name="hebb",
    )(planes, low, low.T, basis_modes)


def finish_kernel(n, rate, coord_count, base, mine, other, out, norms, updated, slots, send, recv):
    rows = base.shape[0]
    width = base.shape[1]
    piece = math.gcd(rows, 256)

    def update(i, sums):
        here = pl.ds(pl.multiple_of(i * piece, piece), piece)
        both = mine[here, :].astype(jnp.float32) + other[here, :].astype(jnp.float32)
        value = base[here, :] + rate * both
        updated[here, :] = value
        return sums + jnp.sum((value * value).reshape(piece // 8, 8, width), axis=0)

    sums = lax.fori_loop(0, rows // piece, update, jnp.zeros((8, width), jnp.float32))
    me = greet(n, "patch")
    slots[me] = sums
    copies = []
    for step in range(1, n):
        copy = pltpu.make_async_remote_copy(
            src_ref=slots.at[me],
            dst_ref=slots.at[me],
            send_sem=send.at[step],
            recv_sem=recv.at[step],
            device_id={"patch": lax.rem(me + step, n)},
            device_id_type=MESH,
        )
        copy.start()
        copies.append(copy)
    for copy in copies:
        copy.wait()
    squares = jnp.sum(jnp.sum(slots[...], axis=0), axis=0, keepdims=True)
    norm = jnp.sqrt(squares / coord_count + 1e-06)
    norms[...] = norm

    def divide(i, _):
        here = pl.ds(pl.multiple_of(i * piece, piece), piece)
        out[here, :] = (updated[here, :] / norm).astype(jnp.bfloat16)
        return 0

    lax.fori_loop(0, rows // piece, divide, 0)


def finished(base, mine, other, rate, coord_count):
    n = lax.axis_size("patch")
    rows, width = base.shape
    return pl.pallas_call(
        functools.partial(finish_kernel, n, rate, coord_count),
        out_shape=(
            jax.ShapeDtypeStruct((rows, width), jnp.bfloat16),
            jax.ShapeDtypeStruct((1, width), jnp.float32),
        ),
        in_specs=[VMEM] * 3,
        out_specs=(VMEM, VMEM),
        scratch_shapes=[
            pltpu.VMEM((rows, width), jnp.float32),
            pltpu.VMEM((n, 8, width), jnp.float32),
            pltpu.SemaphoreType.DMA((n,)),
            pltpu.SemaphoreType.DMA((n,)),
        ],
        compiler_params=pltpu.CompilerParams(
            collective_id=1, has_side_effects=True, vmem_limit_bytes=LIMIT
        ),
        name="finish",
    )(base, mine, other)


def body(subjects, basis_modes, laplace_blocks, columns):
    subject_count, coords, vert_count = subjects.shape
    mode_count = basis_modes.shape[2]
    batch = lax.axis_size("batch")
    coord_count = coords * vert_count * lax.axis_size("patch")
    scale_inv = 1.0 / math.sqrt(coord_count)
    planes = subjects.transpose(1, 0, 2)
    partial_value = lax.dot_general(
        subjects, basis_modes, (((1, 2), (0, 1)), ((), ())), preferred_element_type=jnp.float32
    )
    scores, low = reduce_scores(partial_value, scale_inv)
    base = smoothed(basis_modes, laplace_blocks, columns)
    hebb = hebbian(planes, low, basis_modes, scale_inv)
    other = lax.ppermute(hebb, "batch", [(i, (i + 1) % batch) for i in range(batch)])
    flat = (coords * vert_count, mode_count)
    rate = 4.0 / (subject_count * batch)
    new_modes, norms = finished(
        base.reshape(flat), hebb.reshape(flat), other.reshape(flat), rate, coord_count
    )
    return (scores, new_modes.reshape(coords, vert_count, mode_count), norms.reshape(mode_count))


def solution(mesh):
    placed = (
        P(("groups", "batch"), None, "patch"),
        P(None, ("groups", "patch"), None),
        P("patch", None, None, None),
        P("patch", None),
    )
    return jax.shard_map(
        body,
        mesh=mesh,
        in_specs=placed,
        out_specs=(P(("groups", "batch"), None), P(None, ("groups", "patch"), None), P("groups")),
        check_vma=False,
    )
```

```python
import functools
import math

import jax
import jax.numpy as jnp
from jax import lax
from jax.experimental import pallas as pl
from jax.experimental.pallas import tpu as pltpu
from jax.sharding import PartitionSpec as P

GHOST = 4
MESH = pl.DeviceIdType.MESH
VMEM = pl.BlockSpec(memory_space=pltpu.VMEM)
ANY = pl.BlockSpec(memory_space=pl.ANY)
SMEM = pl.BlockSpec(memory_space=pltpu.SMEM)
LIMIT = 60 * 1024 * 1024


def greet(axes):
    barrier = pltpu.get_barrier_semaphore()
    peers = 0
    for axis in axes:
        n, me = lax.axis_size(axis), lax.axis_index(axis)
        for step in range(1, n):
            pl.semaphore_signal(
                barrier, inc=1, device_id={axis: lax.rem(me + step, n)}, device_id_type=MESH
            )
        peers += n - 1
    pl.semaphore_wait(barrier, peers)


def sum_kernel(
    n, scale, reach, part_ref, modes, blocks, columns, out_ref, low_ref, turned_ref,
    after, before, back_blocks, back_cols, land, full, send_a, recv_a, send_b, recv_b, send_c, recv_c,
):
    greet(("patch",))
    me = lax.axis_index("patch")
    rows = part_ref.shape[0] // n

    def start(source, target, to, send, recv):
        copy = pltpu.make_async_remote_copy(
            src_ref=source,
            dst_ref=target,
            send_sem=send,
            recv_sem=recv,
            device_id={"patch": to},
            device_id_type=MESH,
        )
        copy.start()
        return copy

    copies = []
    for step in range(1, n):
        to = lax.rem(me + step, n)
        source = part_ref.at[pl.ds(pl.multiple_of(to * rows, rows), rows)]
        copies.append(start(source, land.at[step], to, send_a.at[step], recv_a.at[step]))
    following, previous = lax.rem(me + 1, n), lax.rem(me + n - 1, n)
    verts, count = modes.shape[1], blocks.shape[0]
    edges = []
    for index, (source, target, to) in enumerate((
        (blocks.at[pl.ds(count - GHOST, GHOST)], back_blocks, following),
        (columns, back_cols, following),
        (modes.at[:, pl.ds(verts - reach, reach)], before, following),
        (modes.at[:, pl.ds(0, reach)], after, previous),
    )):
        edges.append(start(source, target, to, send_c.at[index], recv_c.at[index]))
    own = pl.ds(pl.multiple_of(me * rows, rows), rows)
    total = part_ref[own, :]
    for step, copy in enumerate(copies, 1):
        copy.wait()
        total = total + land[step]
    full[own, :] = (total * scale).astype(jnp.bfloat16)
    copies = []
    for step in range(1, n):
        to = lax.rem(me + step, n)
        copies.append(start(full.at[own], full.at[own], to, send_b.at[step], recv_b.at[step]))
    for copy in copies:
        copy.wait()
    scores = full[...].astype(jnp.float32)
    out_ref[...] = scores
    low_ref[...] = full[...]
    turned_ref[...] = scores.T.astype(jnp.bfloat16)
    for copy in edges:
        copy.wait()


def reduce_scores(partial_value, basis_modes, laplace_blocks, columns, scale):
    n = lax.axis_size("patch")
    rows, width = partial_value.shape
    coords = basis_modes.shape[0]
    per_row, side = laplace_blocks.shape[1:3]
    reach = GHOST * side
    chunk = pltpu.VMEM((n, rows // n, width), jnp.float32)
    return pl.pallas_call(
        functools.partial(sum_kernel, n, scale, reach),
        out_shape=(
            jax.ShapeDtypeStruct((rows, width), jnp.float32),
            jax.ShapeDtypeStruct((rows, width), jnp.bfloat16),
            jax.ShapeDtypeStruct((width, rows), jnp.bfloat16),
            jax.ShapeDtypeStruct((coords, reach, width), jnp.bfloat16),
            jax.ShapeDtypeStruct((coords, reach, width), jnp.bfloat16),
            jax.ShapeDtypeStruct((GHOST, per_row, side, side), jnp.bfloat16),
            jax.ShapeDtypeStruct(columns.shape, columns.dtype),
        ),
        in_specs=[VMEM, ANY, ANY, VMEM],
        out_specs=(VMEM, VMEM, VMEM, ANY, ANY, ANY, VMEM),
        scratch_shapes=[chunk, pltpu.VMEM((rows, width), jnp.bfloat16)]
        + [pltpu.SemaphoreType.DMA((n,))] * 4
        + [pltpu.SemaphoreType.DMA((4,))] * 2,
        compiler_params=pltpu.CompilerParams(collective_id=0, has_side_effects=True),
        name="reduce_scores",
    )(partial_value, basis_modes, laplace_blocks, columns)


def smooth_kernel(cols, back_cols, blocks, back_blocks, modes, after, before, out, wide, acc):
    count, per_row, side, _ = blocks.shape
    coords, verts, width = modes.shape
    reach = after.shape[1]
    ones = jnp.ones((wide.shape[0], width), jnp.bfloat16)
    for c in range(coords):
        lanes = slice(c * width, (c + 1) * width)
        wide[:verts, lanes] = modes[c]
        wide[verts : verts + reach, lanes] = after[c]
        wide[verts + reach :, lanes] = before[c]
    wide[:, coords * width :] = ones
    acc[...] = jnp.zeros_like(acc)

    def rows_of(block):
        return pl.ds(pl.multiple_of(block * side, side), side)

    def scatter(joined, block, targets):
        moved = lax.dot_general(
            joined,
            wide[rows_of(block), :],
            (((0,), (0,)), ((), ())),
            preferred_element_type=jnp.float32,
        )
        for slot, target in enumerate(targets):
            acc[rows_of(target), :] += moved[slot * side : (slot + 1) * side]

    group = math.gcd(count, 4)

    def step(outer, _):
        for inner in range(group):
            i = outer * group + inner
            joined = jnp.concatenate([blocks[i, slot] for slot in range(per_row)], axis=1)
            targets = [cols[i, slot] for slot in range(per_row)]
            picked = jnp.concatenate([wide[rows_of(t), :] for t in targets], axis=0)
            acc[rows_of(i), :] += jnp.dot(joined, picked, preferred_element_type=jnp.float32)
            scatter(joined, i, targets)
        return 0

    lax.fori_loop(0, count // group, step, 0)

    def back_step(i, _):
        joined = jnp.concatenate([back_blocks[i, slot] for slot in range(per_row)], axis=1)
        targets = [back_cols[i, slot] for slot in range(per_row)]
        scatter(joined, count + reach // side + i, targets)
        return 0

    lax.fori_loop(0, back_blocks.shape[0], back_step, 0)

    def finish(i, _):
        rows = rows_of(i)
        degree = acc[rows, coords * width :]
        for c in range(coords):
            mode = modes[c, rows, :].astype(jnp.float32)
            out[c, rows, :] = mode - 0.2 * (
                degree * mode - acc[rows, c * width : (c + 1) * width]
            )
        return 0

    lax.fori_loop(0, count, finish, 0)


def smoothed(basis_modes, laplace_blocks, columns, after, before, back_blocks, back_cols):
    count, per_row, side, _ = laplace_blocks.shape
    coords, verts, width = basis_modes.shape
    first = lax.axis_index("patch") * count
    total = count + 2 * GHOST
    cols = columns - first
    back = back_cols[count - GHOST :] - first
    back = jnp.where((back >= 0) & (back < GHOST), back, total - 1)
    return pl.pallas_call(
        smooth_kernel,
        out_shape=jax.ShapeDtypeStruct((coords, verts, width), jnp.float32),
        in_specs=[SMEM, SMEM] + [VMEM] * 5,
        out_specs=VMEM,
        scratch_shapes=[
            pltpu.VMEM((total * side, (coords + 1) * width), jnp.bfloat16),
            pltpu.VMEM((total * side, (coords + 1) * width), jnp.float32),
        ],
        compiler_params=pltpu.CompilerParams(vmem_limit_bytes=LIMIT),
        name="smooth",
    )(cols, back, laplace_blocks, back_blocks, basis_modes, after, before)


def update_kernel(
    scale, rate, coord_count, planes, base, modes, low, turned, out, norms,
    held, updated, both, slots, load, send_h, recv_h, send_n, recv_n,
):
    n, me = lax.axis_size("patch"), lax.axis_index("patch")
    pair, half = lax.axis_size("batch"), lax.axis_index("batch")
    tiles, subjects, tile = held.shape
    coords, verts, width = modes.shape
    per = verts // tile
    loads = []
    for i in range(tiles):
        source = planes.at[i // per, :, pl.ds((i % per) * tile, tile)]
        loads.append(pltpu.make_async_copy(source, held.at[i], load.at[i]))
        loads[-1].start()
    loads.append(pltpu.make_async_copy(base, updated, load.at[tiles]))
    loads[-1].start()
    greet(("patch", "batch"))

    copies = []
    for i in range(tiles):
        mode = modes[i // per, (i % per) * tile : (i % per + 1) * tile, :]
        loads[i].wait()
        recon = lax.dot_general(
            low[...], mode, (((1,), (1,)), ((), ())), preferred_element_type=jnp.float32
        )
        residual = (held[i].astype(jnp.float32) - recon * scale).astype(jnp.bfloat16)
        hebb = jnp.dot(turned[...], residual, preferred_element_type=jnp.float32)
        rows = pl.ds(i * tile, tile)
        both[half, rows, :] = hebb.T.astype(jnp.bfloat16)
        for step in range(1, pair):
            copy = pltpu.make_async_remote_copy(
                src_ref=both.at[half, rows],
                dst_ref=both.at[half, rows],
                send_sem=send_h.at[step, i],
                recv_sem=recv_h.at[step, i],
                device_id={"batch": lax.rem(half + step, pair)},
                device_id_type=MESH,
            )
            copy.start()
            copies.append(copy)
    for copy in copies:
        copy.wait()
    loads[tiles].wait()

    piece = math.gcd(coords * verts, 256)

    def update(i, sums):
        here = pl.ds(pl.multiple_of(i * piece, piece), piece)
        hebb = both[0, here, :].astype(jnp.float32)
        for other in range(1, pair):
            hebb = hebb + both[other, here, :].astype(jnp.float32)
        value = updated[here, :] + rate * hebb
        updated[here, :] = value
        return sums + jnp.sum((value * value).reshape(piece // 8, 8, width), axis=0)

    count = coords * verts // piece
    slots[me] = lax.fori_loop(0, count, update, jnp.zeros((8, width), jnp.float32))
    copies = []
    for step in range(1, n):
        copy = pltpu.make_async_remote_copy(
            src_ref=slots.at[me],
            dst_ref=slots.at[me],
            send_sem=send_n.at[step],
            recv_sem=recv_n.at[step],
            device_id={"patch": lax.rem(me + step, n)},
            device_id_type=MESH,
        )
        copy.start()
        copies.append(copy)
    for copy in copies:
        copy.wait()
    squares = jnp.sum(jnp.sum(slots[...], axis=0), axis=0, keepdims=True)
    norm = jnp.sqrt(squares / coord_count + 1e-06)
    norms[...] = norm
    inverse = 1.0 / norm

    def divide(i, _):
        here = pl.ds(pl.multiple_of(i * piece, piece), piece)
        out[here, :] = (updated[here, :] * inverse).astype(jnp.bfloat16)
        return 0

    lax.fori_loop(0, count, divide, 0)


def updated_modes(planes, base, basis_modes, low, turned, scale, rate, coord_count):
    n, pair = lax.axis_size("patch"), lax.axis_size("batch")
    coords, subjects, verts = planes.shape
    width = basis_modes.shape[2]
    rows = coords * verts
    tile = math.gcd(verts, 512)
    tiles = rows // tile
    return pl.pallas_call(
        functools.partial(update_kernel, scale, rate, coord_count),
        out_shape=(
            jax.ShapeDtypeStruct((rows, width), jnp.bfloat16),
            jax.ShapeDtypeStruct((1, width), jnp.float32),
        ),
        in_specs=[ANY, ANY, VMEM, VMEM, VMEM],
        out_specs=(VMEM, VMEM),
        scratch_shapes=[
            pltpu.VMEM((tiles, subjects, tile), jnp.bfloat16),
            pltpu.VMEM((rows, width), jnp.float32),
            pltpu.VMEM((pair, rows, width), jnp.bfloat16),
            pltpu.VMEM((n, 8, width), jnp.float32),
            pltpu.SemaphoreType.DMA((tiles + 1,)),
            pltpu.SemaphoreType.DMA((pair, tiles)),
            pltpu.SemaphoreType.DMA((pair, tiles)),
            pltpu.SemaphoreType.DMA((n,)),
            pltpu.SemaphoreType.DMA((n,)),
        ],
        compiler_params=pltpu.CompilerParams(
            collective_id=1, has_side_effects=True, vmem_limit_bytes=LIMIT
        ),
        name="update",
    )(planes, base.reshape(rows, width), basis_modes, low, turned)


def body(subjects, basis_modes, laplace_blocks, columns):
    subject_count, coords, vert_count = subjects.shape
    mode_count = basis_modes.shape[2]
    batch = lax.axis_size("batch")
    coord_count = coords * vert_count * lax.axis_size("patch")
    scale_inv = 1.0 / math.sqrt(coord_count)
    planes = subjects.transpose(1, 0, 2)
    partial_value = lax.dot_general(
        subjects, basis_modes, (((1, 2), (0, 1)), ((), ())), preferred_element_type=jnp.float32
    )
    scores, low, turned, *edges = reduce_scores(
        partial_value, basis_modes, laplace_blocks, columns, scale_inv
    )
    base = smoothed(basis_modes, laplace_blocks, columns, *edges)
    rate = 4.0 / (subject_count * batch)
    new_modes, norms = updated_modes(
        planes, base, basis_modes, low, turned, scale_inv, rate, coord_count
    )
    return (scores, new_modes.reshape(coords, vert_count, mode_count), norms.reshape(mode_count))


def solution(mesh):
    placed = (
        P(("groups", "batch"), None, "patch"),
        P(None, ("groups", "patch"), None),
        P("patch", None, None, None),
        P("patch", None),
    )
    return jax.shard_map(
        body,
        mesh=mesh,
        in_specs=placed,
        out_specs=(P(("groups", "batch"), None), P(None, ("groups", "patch"), None), P("groups")),
        check_vma=False,
    )
```

```python
import functools
import math

import jax
import jax.numpy as jnp
from jax import lax
from jax.experimental import pallas as pl
from jax.experimental.pallas import tpu as pltpu
from jax.sharding import PartitionSpec as P

GHOST = 4
MESH = pl.DeviceIdType.MESH
VMEM = pl.BlockSpec(memory_space=pltpu.VMEM)
ANY = pl.BlockSpec(memory_space=pl.ANY)
SMEM = pl.BlockSpec(memory_space=pltpu.SMEM)
LIMIT = 60 * 1024 * 1024


def greet(axes):
    barrier = pltpu.get_barrier_semaphore()
    peers = 0
    for axis in axes:
        n, me = lax.axis_size(axis), lax.axis_index(axis)
        for step in range(1, n):
            pl.semaphore_signal(
                barrier, inc=1, device_id={axis: lax.rem(me + step, n)}, device_id_type=MESH
            )
        peers += n - 1
    pl.semaphore_wait(barrier, peers)


def sum_kernel(
    n, scale, part_ref, modes, out_ref, low_ref, turned_ref, after,
    land, full, send_a, recv_a, send_b, recv_b, send_c, recv_c,
):
    greet(("patch",))
    me = lax.axis_index("patch")
    rows = part_ref.shape[0] // n

    def start(source, target, to, send, recv):
        copy = pltpu.make_async_remote_copy(
            src_ref=source,
            dst_ref=target,
            send_sem=send,
            recv_sem=recv,
            device_id={"patch": to},
            device_id_type=MESH,
        )
        copy.start()
        return copy

    copies = []
    for step in range(1, n):
        to = lax.rem(me + step, n)
        source = part_ref.at[pl.ds(pl.multiple_of(to * rows, rows), rows)]
        copies.append(start(source, land.at[step], to, send_a.at[step], recv_a.at[step]))
    edge = pltpu.make_async_remote_copy(
        src_ref=modes.at[:, pl.ds(0, after.shape[1])],
        dst_ref=after,
        send_sem=send_c,
        recv_sem=recv_c,
        device_id={"patch": lax.rem(me + n - 1, n)},
        device_id_type=MESH,
    )

    @pl.when(me > 0)
    def _():
        edge.start()

    @pl.when(me == n - 1)
    def _():
        after[...] = jnp.zeros_like(after)

    own = pl.ds(pl.multiple_of(me * rows, rows), rows)
    total = part_ref[own, :]
    for step, copy in enumerate(copies, 1):
        copy.wait()
        total = total + land[step]
    full[own, :] = (total * scale).astype(jnp.bfloat16)
    copies = []
    for step in range(1, n):
        to = lax.rem(me + step, n)
        copies.append(start(full.at[own], full.at[own], to, send_b.at[step], recv_b.at[step]))
    for copy in copies:
        copy.wait()
    scores = full[...].astype(jnp.float32)
    out_ref[...] = scores
    low_ref[...] = full[...]
    turned_ref[...] = scores.T.astype(jnp.bfloat16)

    @pl.when(me > 0)
    def _():
        edge.wait_send()

    @pl.when(me < n - 1)
    def _():
        edge.wait_recv()


def reduce_scores(partial_value, basis_modes, reach, scale):
    n = lax.axis_size("patch")
    rows, width = partial_value.shape
    coords = basis_modes.shape[0]
    chunk = pltpu.VMEM((n, rows // n, width), jnp.float32)
    return pl.pallas_call(
        functools.partial(sum_kernel, n, scale),
        out_shape=(
            jax.ShapeDtypeStruct((rows, width), jnp.float32),
            jax.ShapeDtypeStruct((rows, width), jnp.bfloat16),
            jax.ShapeDtypeStruct((width, rows), jnp.bfloat16),
            jax.ShapeDtypeStruct((coords, reach, width), jnp.bfloat16),
        ),
        in_specs=[VMEM, ANY],
        out_specs=(VMEM,) * 4,
        scratch_shapes=[chunk, pltpu.VMEM((rows, width), jnp.bfloat16)]
        + [pltpu.SemaphoreType.DMA((n,))] * 4
        + [pltpu.SemaphoreType.DMA] * 2,
        compiler_params=pltpu.CompilerParams(collective_id=0, has_side_effects=True),
        name="reduce_scores",
    )(partial_value, basis_modes)


def smooth_kernel(cols, blocks, modes, after, out, carry, wide, acc):
    count, per_row, side, _ = blocks.shape
    coords, verts, width = modes.shape
    ones = jnp.ones((wide.shape[0], width), jnp.bfloat16)
    for c in range(coords):
        lanes = slice(c * width, (c + 1) * width)
        wide[:verts, lanes] = modes[c]
        wide[verts:, lanes] = after[c]
    wide[:, coords * width :] = ones
    acc[...] = jnp.zeros_like(acc)

    def rows_of(block):
        return pl.ds(pl.multiple_of(block * side, side), side)

    def scatter(joined, block, targets):
        moved = lax.dot_general(
            joined,
            wide[rows_of(block), :],
            (((0,), (0,)), ((), ())),
            preferred_element_type=jnp.float32,
        )
        for slot, target in enumerate(targets):
            acc[rows_of(target), :] += moved[slot * side : (slot + 1) * side]

    group = math.gcd(count, 4)

    def step(outer, _):
        for inner in range(group):
            i = outer * group + inner
            joined = jnp.concatenate([blocks[i, slot] for slot in range(per_row)], axis=1)
            targets = [cols[i, slot] for slot in range(per_row)]
            picked = jnp.concatenate([wide[rows_of(t), :] for t in targets], axis=0)
            acc[rows_of(i), :] += jnp.dot(joined, picked, preferred_element_type=jnp.float32)
            scatter(joined, i, targets)
        return 0

    lax.fori_loop(0, count // group, step, 0)

    carry[...] = acc[verts:, :].astype(jnp.bfloat16)

    def finish(i, _):
        rows = rows_of(i)
        degree = acc[rows, coords * width :]
        for c in range(coords):
            mode = modes[c, rows, :].astype(jnp.float32)
            out[c, rows, :] = mode - 0.2 * (
                degree * mode - acc[rows, c * width : (c + 1) * width]
            )
        return 0

    lax.fori_loop(0, count, finish, 0)


def smoothed(basis_modes, laplace_blocks, columns, after):
    count, per_row, side, _ = laplace_blocks.shape
    coords, verts, width = basis_modes.shape
    cols = columns - lax.axis_index("patch") * count
    reach = after.shape[1]
    lanes = (coords + 1) * width
    return pl.pallas_call(
        smooth_kernel,
        out_shape=(
            jax.ShapeDtypeStruct((coords, verts, width), jnp.float32),
            jax.ShapeDtypeStruct((reach, lanes), jnp.bfloat16),
        ),
        in_specs=[SMEM] + [VMEM] * 3,
        out_specs=(VMEM, VMEM),
        scratch_shapes=[
            pltpu.VMEM((verts + reach, lanes), jnp.bfloat16),
            pltpu.VMEM((verts + reach, lanes), jnp.float32),
        ],
        compiler_params=pltpu.CompilerParams(vmem_limit_bytes=LIMIT),
        name="smooth",
    )(cols, laplace_blocks, basis_modes, after)


def update_kernel(
    scale, rate, coord_count, planes, base, modes, low, turned, carry, out, norms,
    held, updated, both, slots, extra, load, send_h, recv_h, send_n, recv_n, send_c, recv_c,
):
    n, me = lax.axis_size("patch"), lax.axis_index("patch")
    pair, half = lax.axis_size("batch"), lax.axis_index("batch")
    tiles, subjects, tile = held.shape
    coords, verts, width = modes.shape
    per = verts // tile
    loads = []
    for i in range(tiles):
        source = planes.at[i // per, :, pl.ds((i % per) * tile, tile)]
        loads.append(pltpu.make_async_copy(source, held.at[i], load.at[i]))
        loads[-1].start()
    loads.append(pltpu.make_async_copy(base, updated, load.at[tiles]))
    loads[-1].start()
    greet(("patch", "batch"))
    edge = pltpu.make_async_remote_copy(
        src_ref=carry,
        dst_ref=extra,
        send_sem=send_c,
        recv_sem=recv_c,
        device_id={"patch": lax.rem(me + 1, n)},
        device_id_type=MESH,
    )

    @pl.when(me < n - 1)
    def _():
        edge.start()

    @pl.when(me == 0)
    def _():
        extra[...] = jnp.zeros_like(extra)

    copies = []
    for i in range(tiles):
        mode = modes[i // per, (i % per) * tile : (i % per + 1) * tile, :]
        loads[i].wait()
        recon = lax.dot_general(
            low[...], mode, (((1,), (1,)), ((), ())), preferred_element_type=jnp.float32
        )
        residual = (held[i].astype(jnp.float32) - recon * scale).astype(jnp.bfloat16)
        hebb = jnp.dot(turned[...], residual, preferred_element_type=jnp.float32)
        rows = pl.ds(i * tile, tile)
        both[half, rows, :] = hebb.T.astype(jnp.bfloat16)
        for step in range(1, pair):
            copy = pltpu.make_async_remote_copy(
                src_ref=both.at[half, rows],
                dst_ref=both.at[half, rows],
                send_sem=send_h.at[step, i],
                recv_sem=recv_h.at[step, i],
                device_id={"batch": lax.rem(half + step, pair)},
                device_id_type=MESH,
            )
            copy.start()
            copies.append(copy)
    loads[tiles].wait()

    @pl.when(me < n - 1)
    def _():
        edge.wait_send()

    @pl.when(me > 0)
    def _():
        edge.wait_recv()

    reach = extra.shape[0]
    degree = extra[:, coords * width :].astype(jnp.float32)
    for c in range(coords):
        mode = modes[c, :reach, :].astype(jnp.float32)
        terms = degree * mode - extra[:, c * width : (c + 1) * width].astype(jnp.float32)
        updated[c * verts : c * verts + reach, :] += -0.2 * terms
    for copy in copies:
        copy.wait()

    piece = math.gcd(coords * verts, 256)

    def update(i, sums):
        here = pl.ds(pl.multiple_of(i * piece, piece), piece)
        hebb = both[0, here, :].astype(jnp.float32)
        for other in range(1, pair):
            hebb = hebb + both[other, here, :].astype(jnp.float32)
        value = updated[here, :] + rate * hebb
        updated[here, :] = value
        return sums + jnp.sum((value * value).reshape(piece // 8, 8, width), axis=0)

    count = coords * verts // piece
    slots[me] = lax.fori_loop(0, count, update, jnp.zeros((8, width), jnp.float32))
    copies = []
    for step in range(1, n):
        copy = pltpu.make_async_remote_copy(
            src_ref=slots.at[me],
            dst_ref=slots.at[me],
            send_sem=send_n.at[step],
            recv_sem=recv_n.at[step],
            device_id={"patch": lax.rem(me + step, n)},
            device_id_type=MESH,
        )
        copy.start()
        copies.append(copy)
    for copy in copies:
        copy.wait()
    squares = jnp.sum(jnp.sum(slots[...], axis=0), axis=0, keepdims=True)
    norm = jnp.sqrt(squares / coord_count + 1e-06)
    norms[...] = norm
    inverse = 1.0 / norm

    def divide(i, _):
        here = pl.ds(pl.multiple_of(i * piece, piece), piece)
        out[here, :] = (updated[here, :] * inverse).astype(jnp.bfloat16)
        return 0

    lax.fori_loop(0, count, divide, 0)


def updated_modes(planes, base, carry, basis_modes, low, turned, scale, rate, coord_count):
    n, pair = lax.axis_size("patch"), lax.axis_size("batch")
    coords, subjects, verts = planes.shape
    width = basis_modes.shape[2]
    rows = coords * verts
    tile = math.gcd(verts, 512)
    tiles = rows // tile
    return pl.pallas_call(
        functools.partial(update_kernel, scale, rate, coord_count),
        out_shape=(
            jax.ShapeDtypeStruct((rows, width), jnp.bfloat16),
            jax.ShapeDtypeStruct((1, width), jnp.float32),
        ),
        in_specs=[ANY, ANY] + [VMEM] * 4,
        out_specs=(VMEM, VMEM),
        scratch_shapes=[
            pltpu.VMEM((tiles, subjects, tile), jnp.bfloat16),
            pltpu.VMEM((rows, width), jnp.float32),
            pltpu.VMEM((pair, rows, width), jnp.bfloat16),
            pltpu.VMEM((n, 8, width), jnp.float32),
            pltpu.VMEM(carry.shape, carry.dtype),
            pltpu.SemaphoreType.DMA((tiles + 1,)),
            pltpu.SemaphoreType.DMA((pair, tiles)),
            pltpu.SemaphoreType.DMA((pair, tiles)),
            pltpu.SemaphoreType.DMA((n,)),
            pltpu.SemaphoreType.DMA((n,)),
            pltpu.SemaphoreType.DMA,
            pltpu.SemaphoreType.DMA,
        ],
        compiler_params=pltpu.CompilerParams(
            collective_id=1, has_side_effects=True, vmem_limit_bytes=LIMIT
        ),
        name="update",
    )(planes, base.reshape(rows, width), basis_modes, low, turned, carry)


def body(subjects, basis_modes, laplace_blocks, columns):
    subject_count, coords, vert_count = subjects.shape
    mode_count = basis_modes.shape[2]
    batch = lax.axis_size("batch")
    coord_count = coords * vert_count * lax.axis_size("patch")
    scale_inv = 1.0 / math.sqrt(coord_count)
    planes = subjects.transpose(1, 0, 2)
    partial_value = lax.dot_general(
        subjects, basis_modes, (((1, 2), (0, 1)), ((), ())), preferred_element_type=jnp.float32
    )
    reach = GHOST * laplace_blocks.shape[2]
    scores, low, turned, after = reduce_scores(partial_value, basis_modes, reach, scale_inv)
    base, carry = smoothed(basis_modes, laplace_blocks, columns, after)
    rate = 4.0 / (subject_count * batch)
    new_modes, norms = updated_modes(
        planes, base, carry, basis_modes, low, turned, scale_inv, rate, coord_count
    )
    return (scores, new_modes.reshape(coords, vert_count, mode_count), norms.reshape(mode_count))


def solution(mesh):
    placed = (
        P(("groups", "batch"), None, "patch"),
        P(None, ("groups", "patch"), None),
        P("patch", None, None, None),
        P("patch", None),
    )
    return jax.shard_map(
        body,
        mesh=mesh,
        in_specs=placed,
        out_specs=(P(("groups", "batch"), None), P(None, ("groups", "patch"), None), P("groups")),
        check_vma=False,
    )
```

```python
import functools
import math

import jax
import jax.numpy as jnp
from jax import lax
from jax.experimental import pallas as pl
from jax.experimental.pallas import tpu as pltpu
from jax.sharding import PartitionSpec as P

GHOST = 4
MESH = pl.DeviceIdType.MESH
VMEM = pl.BlockSpec(memory_space=pltpu.VMEM)
ANY = pl.BlockSpec(memory_space=pl.ANY)
SMEM = pl.BlockSpec(memory_space=pltpu.SMEM)
LIMIT = 60 * 1024 * 1024


def greet(axes):
    barrier = pltpu.get_barrier_semaphore()
    peers = 0
    for axis in axes:
        n, me = lax.axis_size(axis), lax.axis_index(axis)
        for step in range(1, n):
            pl.semaphore_signal(
                barrier, inc=1, device_id={axis: lax.rem(me + step, n)}, device_id_type=MESH
            )
        peers += n - 1
    pl.semaphore_wait(barrier, peers)


def sum_kernel(
    n, scale, part_ref, modes, low_ref, turned_ref, after,
    land, full, send_a, recv_a, send_b, recv_b, send_c, recv_c,
):
    greet(("patch",))
    me = lax.axis_index("patch")
    rows = part_ref.shape[0] // n

    def start(source, target, to, send, recv):
        copy = pltpu.make_async_remote_copy(
            src_ref=source,
            dst_ref=target,
            send_sem=send,
            recv_sem=recv,
            device_id={"patch": to},
            device_id_type=MESH,
        )
        copy.start()
        return copy

    copies = []
    for step in range(1, n):
        to = lax.rem(me + step, n)
        source = part_ref.at[pl.ds(pl.multiple_of(to * rows, rows), rows)]
        copies.append(start(source, land.at[step], to, send_a.at[step], recv_a.at[step]))
    edge = pltpu.make_async_remote_copy(
        src_ref=modes.at[:, pl.ds(0, after.shape[1])],
        dst_ref=after,
        send_sem=send_c,
        recv_sem=recv_c,
        device_id={"patch": lax.rem(me + n - 1, n)},
        device_id_type=MESH,
    )

    @pl.when(me > 0)
    def _():
        edge.start()

    @pl.when(me == n - 1)
    def _():
        after[...] = jnp.zeros_like(after)

    own = pl.ds(pl.multiple_of(me * rows, rows), rows)
    total = part_ref[own, :]
    for step, copy in enumerate(copies, 1):
        copy.wait()
        total = total + land[step]
    full[own, :] = (total * scale).astype(jnp.bfloat16)
    copies = []
    for step in range(1, n):
        to = lax.rem(me + step, n)
        copies.append(start(full.at[own], full.at[own], to, send_b.at[step], recv_b.at[step]))
    for copy in copies:
        copy.wait()
    low_ref[...] = full[...]
    turned_ref[...] = full[...].astype(jnp.float32).T.astype(jnp.bfloat16)

    @pl.when(me > 0)
    def _():
        edge.wait_send()

    @pl.when(me < n - 1)
    def _():
        edge.wait_recv()


def reduce_scores(partial_value, basis_modes, reach, scale):
    n = lax.axis_size("patch")
    rows, width = partial_value.shape
    coords = basis_modes.shape[0]
    chunk = pltpu.VMEM((n, rows // n, width), jnp.float32)
    return pl.pallas_call(
        functools.partial(sum_kernel, n, scale),
        out_shape=(
            jax.ShapeDtypeStruct((rows, width), jnp.bfloat16),
            jax.ShapeDtypeStruct((width, rows), jnp.bfloat16),
            jax.ShapeDtypeStruct((coords, reach, width), jnp.bfloat16),
        ),
        in_specs=[VMEM, ANY],
        out_specs=(VMEM,) * 3,
        scratch_shapes=[chunk, pltpu.VMEM((rows, width), jnp.bfloat16)]
        + [pltpu.SemaphoreType.DMA((n,))] * 4
        + [pltpu.SemaphoreType.DMA] * 2,
        compiler_params=pltpu.CompilerParams(collective_id=0, has_side_effects=True),
        name="reduce_scores",
    )(partial_value, basis_modes)


def smooth_kernel(cols, blocks, modes, after, low, out, carry, scores, wide, acc):
    count, per_row, side, _ = blocks.shape
    coords, verts, width = modes.shape
    first = lax.axis_index("patch") * count
    scores[...] = low[...].astype(jnp.float32)
    ones = jnp.ones((wide.shape[0], width), jnp.bfloat16)
    for c in range(coords):
        lanes = slice(c * width, (c + 1) * width)
        wide[:verts, lanes] = modes[c]
        wide[verts:, lanes] = after[c]
    wide[:, coords * width :] = ones
    acc[...] = jnp.zeros_like(acc)

    def rows_of(block):
        return pl.ds(pl.multiple_of(block * side, side), side)

    def scatter(joined, block, targets):
        moved = lax.dot_general(
            joined,
            wide[rows_of(block), :],
            (((0,), (0,)), ((), ())),
            preferred_element_type=jnp.float32,
        )
        for slot, target in enumerate(targets):
            acc[rows_of(target), :] += moved[slot * side : (slot + 1) * side]

    group = math.gcd(count, 4)

    def step(outer, _):
        for inner in range(group):
            i = outer * group + inner
            joined = jnp.concatenate([blocks[i, slot] for slot in range(per_row)], axis=1)
            targets = [cols[slot, i] - first for slot in range(per_row)]
            picked = jnp.concatenate([wide[rows_of(t), :] for t in targets], axis=0)
            acc[rows_of(i), :] += jnp.dot(joined, picked, preferred_element_type=jnp.float32)
            scatter(joined, i, targets)
        return 0

    lax.fori_loop(0, count // group, step, 0)

    carry[...] = acc[verts:, :].astype(jnp.bfloat16)

    def finish(i, _):
        rows = rows_of(i)
        degree = acc[rows, coords * width :]
        for c in range(coords):
            mode = modes[c, rows, :].astype(jnp.float32)
            out[c, rows, :] = mode - 0.2 * (
                degree * mode - acc[rows, c * width : (c + 1) * width]
            )
        return 0

    lax.fori_loop(0, count, finish, 0)


def smoothed(basis_modes, laplace_blocks, columns, after, low):
    count, per_row, side, _ = laplace_blocks.shape
    coords, verts, width = basis_modes.shape
    reach = after.shape[1]
    lanes = (coords + 1) * width
    return pl.pallas_call(
        smooth_kernel,
        out_shape=(
            jax.ShapeDtypeStruct((coords, verts, width), jnp.float32),
            jax.ShapeDtypeStruct((reach, lanes), jnp.bfloat16),
            jax.ShapeDtypeStruct(low.shape, jnp.float32),
        ),
        in_specs=[SMEM] + [VMEM] * 4,
        out_specs=(VMEM,) * 3,
        scratch_shapes=[
            pltpu.VMEM((verts + reach, lanes), jnp.bfloat16),
            pltpu.VMEM((verts + reach, lanes), jnp.float32),
        ],
        compiler_params=pltpu.CompilerParams(vmem_limit_bytes=LIMIT),
        name="smooth",
    )(columns.T, laplace_blocks, basis_modes, after, low)


def update_kernel(
    scale, rate, coord_count, planes, base, modes, low, turned, carry, out, norms,
    held, updated, both, slots, extra, load, send_h, recv_h, send_n, recv_n, send_c, recv_c,
):
    n, me = lax.axis_size("patch"), lax.axis_index("patch")
    pair, half = lax.axis_size("batch"), lax.axis_index("batch")
    tiles, subjects, tile = held.shape
    coords, verts, width = modes.shape
    per = verts // tile
    loads = []
    for i in range(tiles):
        source = planes.at[i // per, :, pl.ds((i % per) * tile, tile)]
        loads.append(pltpu.make_async_copy(source, held.at[i], load.at[i]))
        loads[-1].start()
    loads.append(pltpu.make_async_copy(base, updated, load.at[tiles]))
    loads[-1].start()
    greet(("patch", "batch"))
    edge = pltpu.make_async_remote_copy(
        src_ref=carry,
        dst_ref=extra,
        send_sem=send_c,
        recv_sem=recv_c,
        device_id={"patch": lax.rem(me + 1, n)},
        device_id_type=MESH,
    )

    @pl.when(me < n - 1)
    def _():
        edge.start()

    @pl.when(me == 0)
    def _():
        extra[...] = jnp.zeros_like(extra)

    def residual_of(i):
        mode = modes[i // per, (i % per) * tile : (i % per + 1) * tile, :]
        recon = lax.dot_general(
            low[...], mode, (((1,), (1,)), ((), ())), preferred_element_type=jnp.float32
        )
        return (held[i].astype(jnp.float32) - recon * scale).astype(jnp.bfloat16)

    copies, ready = [], None
    for i in range(tiles + 1):
        if i < tiles:
            loads[i].wait()
            residual = residual_of(i)
        if i > 0:
            hebb = jnp.dot(turned[...], ready, preferred_element_type=jnp.float32)
            rows = pl.ds((i - 1) * tile, tile)
            both[half, rows, :] = hebb.T.astype(jnp.bfloat16)
            for step in range(1, pair):
                copy = pltpu.make_async_remote_copy(
                    src_ref=both.at[half, rows],
                    dst_ref=both.at[half, rows],
                    send_sem=send_h.at[step, i - 1],
                    recv_sem=recv_h.at[step, i - 1],
                    device_id={"batch": lax.rem(half + step, pair)},
                    device_id_type=MESH,
                )
                copy.start()
                copies.append(copy)
        ready = residual
    loads[tiles].wait()

    @pl.when(me < n - 1)
    def _():
        edge.wait_send()

    @pl.when(me > 0)
    def _():
        edge.wait_recv()

    reach = extra.shape[0]
    degree = extra[:, coords * width :].astype(jnp.float32)
    for c in range(coords):
        mode = modes[c, :reach, :].astype(jnp.float32)
        terms = degree * mode - extra[:, c * width : (c + 1) * width].astype(jnp.float32)
        updated[c * verts : c * verts + reach, :] += -0.2 * terms
    for copy in copies:
        copy.wait()

    piece = math.gcd(coords * verts, 256)

    def update(i, sums):
        here = pl.ds(pl.multiple_of(i * piece, piece), piece)
        hebb = both[0, here, :].astype(jnp.float32)
        for other in range(1, pair):
            hebb = hebb + both[other, here, :].astype(jnp.float32)
        value = updated[here, :] + rate * hebb
        updated[here, :] = value
        return sums + jnp.sum((value * value).reshape(piece // 8, 8, width), axis=0)

    count = coords * verts // piece
    slots[me] = lax.fori_loop(0, count, update, jnp.zeros((8, width), jnp.float32))
    copies = []
    for step in range(1, n):
        copy = pltpu.make_async_remote_copy(
            src_ref=slots.at[me],
            dst_ref=slots.at[me],
            send_sem=send_n.at[step],
            recv_sem=recv_n.at[step],
            device_id={"patch": lax.rem(me + step, n)},
            device_id_type=MESH,
        )
        copy.start()
        copies.append(copy)
    for copy in copies:
        copy.wait()
    squares = jnp.sum(jnp.sum(slots[...], axis=0), axis=0, keepdims=True)
    norm = jnp.sqrt(squares / coord_count + 1e-06)
    norms[...] = norm
    inverse = 1.0 / norm

    def divide(i, _):
        here = pl.ds(pl.multiple_of(i * piece, piece), piece)
        out[here, :] = (updated[here, :] * inverse).astype(jnp.bfloat16)
        return 0

    lax.fori_loop(0, count, divide, 0)


def updated_modes(planes, base, carry, basis_modes, low, turned, scale, rate, coord_count):
    n, pair = lax.axis_size("patch"), lax.axis_size("batch")
    coords, subjects, verts = planes.shape
    width = basis_modes.shape[2]
    rows = coords * verts
    tile = math.gcd(verts, 512)
    tiles = rows // tile
    return pl.pallas_call(
        functools.partial(update_kernel, scale, rate, coord_count),
        out_shape=(
            jax.ShapeDtypeStruct((rows, width), jnp.bfloat16),
            jax.ShapeDtypeStruct((1, width), jnp.float32),
        ),
        in_specs=[ANY, ANY] + [VMEM] * 4,
        out_specs=(VMEM, VMEM),
        scratch_shapes=[
            pltpu.VMEM((tiles, subjects, tile), jnp.bfloat16),
            pltpu.VMEM((rows, width), jnp.float32),
            pltpu.VMEM((pair, rows, width), jnp.bfloat16),
            pltpu.VMEM((n, 8, width), jnp.float32),
            pltpu.VMEM(carry.shape, carry.dtype),
            pltpu.SemaphoreType.DMA((tiles + 1,)),
            pltpu.SemaphoreType.DMA((pair, tiles)),
            pltpu.SemaphoreType.DMA((pair, tiles)),
            pltpu.SemaphoreType.DMA((n,)),
            pltpu.SemaphoreType.DMA((n,)),
            pltpu.SemaphoreType.DMA,
            pltpu.SemaphoreType.DMA,
        ],
        compiler_params=pltpu.CompilerParams(
            collective_id=1, has_side_effects=True, vmem_limit_bytes=LIMIT
        ),
        name="update",
    )(planes, base.reshape(rows, width), basis_modes, low, turned, carry)


def body(subjects, basis_modes, laplace_blocks, columns):
    subject_count, coords, vert_count = subjects.shape
    mode_count = basis_modes.shape[2]
    batch = lax.axis_size("batch")
    coord_count = coords * vert_count * lax.axis_size("patch")
    scale_inv = 1.0 / math.sqrt(coord_count)
    planes = subjects.transpose(1, 0, 2)
    partial_value = lax.dot_general(
        subjects, basis_modes, (((1, 2), (0, 1)), ((), ())), preferred_element_type=jnp.float32
    )
    reach = GHOST * laplace_blocks.shape[2]
    low, turned, after = reduce_scores(partial_value, basis_modes, reach, scale_inv)
    base, carry, scores = smoothed(basis_modes, laplace_blocks, columns, after, low)
    rate = 4.0 / (subject_count * batch)
    new_modes, norms = updated_modes(
        planes, base, carry, basis_modes, low, turned, scale_inv, rate, coord_count
    )
    return (scores, new_modes.reshape(coords, vert_count, mode_count), norms.reshape(mode_count))


def solution(mesh):
    placed = (
        P(("groups", "batch"), None, "patch"),
        P(None, ("groups", "patch"), None),
        P("patch", None, None, None),
        P("patch", None),
    )
    return jax.shard_map(
        body,
        mesh=mesh,
        in_specs=placed,
        out_specs=(P(("groups", "batch"), None), P(None, ("groups", "patch"), None), P("groups")),
        check_vma=False,
    )
```

```python
import functools
import math

import jax
import jax.numpy as jnp
from jax import lax
from jax.experimental import pallas as pl
from jax.experimental.pallas import tpu as pltpu
from jax.sharding import PartitionSpec as P

GHOST = 4
MESH = pl.DeviceIdType.MESH
VMEM = pl.BlockSpec(memory_space=pltpu.VMEM)
ANY = pl.BlockSpec(memory_space=pl.ANY)
SMEM = pl.BlockSpec(memory_space=pltpu.SMEM)
LIMIT = 60 * 1024 * 1024


def greet(axes):
    barrier = pltpu.get_barrier_semaphore()
    peers = 0
    for axis in axes:
        n, me = lax.axis_size(axis), lax.axis_index(axis)
        for step in range(1, n):
            pl.semaphore_signal(
                barrier, inc=1, device_id={axis: lax.rem(me + step, n)}, device_id_type=MESH
            )
        peers += n - 1
    pl.semaphore_wait(barrier, peers)


def sum_kernel(
    n, scale, part_ref, modes, low_ref, turned_ref, after,
    land, full, send_a, recv_a, send_b, recv_b, send_c, recv_c,
):
    greet(("patch",))
    me = lax.axis_index("patch")
    rows = part_ref.shape[0] // n

    def start(source, target, to, send, recv):
        copy = pltpu.make_async_remote_copy(
            src_ref=source,
            dst_ref=target,
            send_sem=send,
            recv_sem=recv,
            device_id={"patch": to},
            device_id_type=MESH,
        )
        copy.start()
        return copy

    copies = []
    for step in range(1, n):
        to = lax.rem(me + step, n)
        source = part_ref.at[pl.ds(pl.multiple_of(to * rows, rows), rows)]
        copies.append(start(source, land.at[step], to, send_a.at[step], recv_a.at[step]))
    edge = pltpu.make_async_remote_copy(
        src_ref=modes.at[:, pl.ds(0, after.shape[1])],
        dst_ref=after,
        send_sem=send_c,
        recv_sem=recv_c,
        device_id={"patch": lax.rem(me + n - 1, n)},
        device_id_type=MESH,
    )

    @pl.when(me > 0)
    def _():
        edge.start()

    @pl.when(me == n - 1)
    def _():
        after[...] = jnp.zeros_like(after)

    own = pl.ds(pl.multiple_of(me * rows, rows), rows)
    total = part_ref[own, :]
    for step, copy in enumerate(copies, 1):
        copy.wait()
        total = total + land[step]
    full[own, :] = (total * scale).astype(jnp.bfloat16)
    copies = []
    for step in range(1, n):
        to = lax.rem(me + step, n)
        copies.append(start(full.at[own], full.at[own], to, send_b.at[step], recv_b.at[step]))
    for copy in copies:
        copy.wait()
    low_ref[...] = full[...]
    turned_ref[...] = full[...].astype(jnp.float32).T.astype(jnp.bfloat16)

    @pl.when(me > 0)
    def _():
        edge.wait_send()

    @pl.when(me < n - 1)
    def _():
        edge.wait_recv()


def reduce_scores(partial_value, basis_modes, reach, scale):
    n = lax.axis_size("patch")
    rows, width = partial_value.shape
    coords = basis_modes.shape[0]
    chunk = pltpu.VMEM((n, rows // n, width), jnp.float32)
    return pl.pallas_call(
        functools.partial(sum_kernel, n, scale),
        out_shape=(
            jax.ShapeDtypeStruct((rows, width), jnp.bfloat16),
            jax.ShapeDtypeStruct((width, rows), jnp.bfloat16),
            jax.ShapeDtypeStruct((coords, reach, width), jnp.bfloat16),
        ),
        in_specs=[VMEM, ANY],
        out_specs=(VMEM,) * 3,
        scratch_shapes=[chunk, pltpu.VMEM((rows, width), jnp.bfloat16)]
        + [pltpu.SemaphoreType.DMA((n,))] * 4
        + [pltpu.SemaphoreType.DMA] * 2,
        compiler_params=pltpu.CompilerParams(collective_id=0, has_side_effects=True),
        name="reduce_scores",
    )(partial_value, basis_modes)


def smooth_kernel(cols, blocks, modes, after, low, out, carry, scores, wide, acc):
    count, per_row, side, _ = blocks.shape
    coords, verts, width = modes.shape
    first = lax.axis_index("patch") * count
    scores[...] = low[...].astype(jnp.float32)
    ones = jnp.ones((wide.shape[0], width), jnp.bfloat16)
    for c in range(coords):
        lanes = slice(c * width, (c + 1) * width)
        wide[:verts, lanes] = modes[c]
        wide[verts:, lanes] = after[c]
    wide[:, coords * width :] = ones
    acc[...] = jnp.zeros_like(acc)

    def rows_of(block):
        return pl.ds(pl.multiple_of(block * side, side), side)

    def scatter(joined, block, targets):
        moved = lax.dot_general(
            joined,
            wide[rows_of(block), :],
            (((0,), (0,)), ((), ())),
            preferred_element_type=jnp.float32,
        )
        for slot, target in enumerate(targets):
            acc[rows_of(target), :] += moved[slot * side : (slot + 1) * side]

    group = math.gcd(count, 8)

    def step(outer, _):
        for inner in range(group):
            i = outer * group + inner
            joined = jnp.concatenate([blocks[i, slot] for slot in range(per_row)], axis=1)
            targets = [cols[slot, i] - first for slot in range(per_row)]
            picked = jnp.concatenate([wide[rows_of(t), :] for t in targets], axis=0)
            acc[rows_of(i), :] += jnp.dot(joined, picked, preferred_element_type=jnp.float32)
            scatter(joined, i, targets)
        return 0

    lax.fori_loop(0, count // group, step, 0)

    carry[...] = acc[verts:, :].astype(jnp.bfloat16)

    def finish(i, _):
        rows = rows_of(i)
        degree = acc[rows, coords * width :]
        for c in range(coords):
            mode = modes[c, rows, :].astype(jnp.float32)
            out[c, rows, :] = mode - 0.2 * (
                degree * mode - acc[rows, c * width : (c + 1) * width]
            )
        return 0

    lax.fori_loop(0, count, finish, 0)


def smoothed(basis_modes, laplace_blocks, columns, after, low):
    count, per_row, side, _ = laplace_blocks.shape
    coords, verts, width = basis_modes.shape
    reach = after.shape[1]
    lanes = (coords + 1) * width
    return pl.pallas_call(
        smooth_kernel,
        out_shape=(
            jax.ShapeDtypeStruct((coords, verts, width), jnp.float32),
            jax.ShapeDtypeStruct((reach, lanes), jnp.bfloat16),
            jax.ShapeDtypeStruct(low.shape, jnp.float32),
        ),
        in_specs=[SMEM] + [VMEM] * 4,
        out_specs=(VMEM,) * 3,
        scratch_shapes=[
            pltpu.VMEM((verts + reach, lanes), jnp.bfloat16),
            pltpu.VMEM((verts + reach, lanes), jnp.float32),
        ],
        compiler_params=pltpu.CompilerParams(vmem_limit_bytes=LIMIT),
        name="smooth",
    )(columns.T, laplace_blocks, basis_modes, after, low)


def update_kernel(
    scale, rate, coord_count, planes, base, modes, low, turned, carry, out, norms,
    held, updated, both, slots, extra, load, send_h, recv_h, send_n, recv_n, send_c, recv_c,
):
    n, me = lax.axis_size("patch"), lax.axis_index("patch")
    pair, half = lax.axis_size("batch"), lax.axis_index("batch")
    tiles, subjects, tile = held.shape
    coords, verts, width = modes.shape
    per = verts // tile
    loads = []
    for i in range(tiles):
        source = planes.at[i // per, :, pl.ds((i % per) * tile, tile)]
        loads.append(pltpu.make_async_copy(source, held.at[i], load.at[i]))
        loads[-1].start()
    loads.append(pltpu.make_async_copy(base, updated, load.at[tiles]))
    loads[-1].start()
    greet(("patch", "batch"))
    edge = pltpu.make_async_remote_copy(
        src_ref=carry,
        dst_ref=extra,
        send_sem=send_c,
        recv_sem=recv_c,
        device_id={"patch": lax.rem(me + 1, n)},
        device_id_type=MESH,
    )

    @pl.when(me < n - 1)
    def _():
        edge.start()

    @pl.when(me == 0)
    def _():
        extra[...] = jnp.zeros_like(extra)

    def residual_of(i):
        mode = modes[i // per, (i % per) * tile : (i % per + 1) * tile, :]
        recon = lax.dot_general(
            low[...], mode, (((1,), (1,)), ((), ())), preferred_element_type=jnp.float32
        )
        return (held[i].astype(jnp.float32) - recon * scale).astype(jnp.bfloat16)

    copies, ready = [], None
    for i in range(tiles + 1):
        if i < tiles:
            loads[i].wait()
            residual = residual_of(i)
        if i > 0:
            hebb = jnp.dot(turned[...], ready, preferred_element_type=jnp.float32)
            rows = pl.ds((i - 1) * tile, tile)
            both[half, rows, :] = hebb.T.astype(jnp.bfloat16)
            for step in range(1, pair):
                copy = pltpu.make_async_remote_copy(
                    src_ref=both.at[half, rows],
                    dst_ref=both.at[half, rows],
                    send_sem=send_h.at[step, i - 1],
                    recv_sem=recv_h.at[step, i - 1],
                    device_id={"batch": lax.rem(half + step, pair)},
                    device_id_type=MESH,
                )
                copy.start()
                copies.append(copy)
        ready = residual
    loads[tiles].wait()

    @pl.when(me < n - 1)
    def _():
        edge.wait_send()

    @pl.when(me > 0)
    def _():
        edge.wait_recv()

    reach = extra.shape[0]
    degree = extra[:, coords * width :].astype(jnp.float32)
    for c in range(coords):
        mode = modes[c, :reach, :].astype(jnp.float32)
        terms = degree * mode - extra[:, c * width : (c + 1) * width].astype(jnp.float32)
        updated[c * verts : c * verts + reach, :] += -0.2 * terms
    for copy in copies:
        copy.wait()

    piece = math.gcd(coords * verts, 256)

    def update(i, sums):
        here = pl.ds(pl.multiple_of(i * piece, piece), piece)
        hebb = both[0, here, :].astype(jnp.float32)
        for other in range(1, pair):
            hebb = hebb + both[other, here, :].astype(jnp.float32)
        value = updated[here, :] + rate * hebb
        updated[here, :] = value
        return sums + jnp.sum((value * value).reshape(piece // 8, 8, width), axis=0)

    count = coords * verts // piece
    slots[me] = lax.fori_loop(0, count, update, jnp.zeros((8, width), jnp.float32))
    copies = []
    for step in range(1, n):
        copy = pltpu.make_async_remote_copy(
            src_ref=slots.at[me],
            dst_ref=slots.at[me],
            send_sem=send_n.at[step],
            recv_sem=recv_n.at[step],
            device_id={"patch": lax.rem(me + step, n)},
            device_id_type=MESH,
        )
        copy.start()
        copies.append(copy)
    for copy in copies:
        copy.wait()
    squares = jnp.sum(jnp.sum(slots[...], axis=0), axis=0, keepdims=True)
    norm = jnp.sqrt(squares / coord_count + 1e-06)
    norms[...] = norm
    inverse = 1.0 / norm

    def divide(i, _):
        here = pl.ds(pl.multiple_of(i * piece, piece), piece)
        out[here, :] = (updated[here, :] * inverse).astype(jnp.bfloat16)
        return 0

    lax.fori_loop(0, count, divide, 0)


def updated_modes(planes, base, carry, basis_modes, low, turned, scale, rate, coord_count):
    n, pair = lax.axis_size("patch"), lax.axis_size("batch")
    coords, subjects, verts = planes.shape
    width = basis_modes.shape[2]
    rows = coords * verts
    tile = math.gcd(verts, 1280)
    tiles = rows // tile
    return pl.pallas_call(
        functools.partial(update_kernel, scale, rate, coord_count),
        out_shape=(
            jax.ShapeDtypeStruct((rows, width), jnp.bfloat16),
            jax.ShapeDtypeStruct((1, width), jnp.float32),
        ),
        in_specs=[ANY, ANY] + [VMEM] * 4,
        out_specs=(VMEM, VMEM),
        scratch_shapes=[
            pltpu.VMEM((tiles, subjects, tile), jnp.bfloat16),
            pltpu.VMEM((rows, width), jnp.float32),
            pltpu.VMEM((pair, rows, width), jnp.bfloat16),
            pltpu.VMEM((n, 8, width), jnp.float32),
            pltpu.VMEM(carry.shape, carry.dtype),
            pltpu.SemaphoreType.DMA((tiles + 1,)),
            pltpu.SemaphoreType.DMA((pair, tiles)),
            pltpu.SemaphoreType.DMA((pair, tiles)),
            pltpu.SemaphoreType.DMA((n,)),
            pltpu.SemaphoreType.DMA((n,)),
            pltpu.SemaphoreType.DMA,
            pltpu.SemaphoreType.DMA,
        ],
        compiler_params=pltpu.CompilerParams(
            collective_id=1, has_side_effects=True, vmem_limit_bytes=LIMIT
        ),
        name="update",
    )(planes, base.reshape(rows, width), basis_modes, low, turned, carry)


def body(subjects, basis_modes, laplace_blocks, columns):
    subject_count, coords, vert_count = subjects.shape
    mode_count = basis_modes.shape[2]
    batch = lax.axis_size("batch")
    coord_count = coords * vert_count * lax.axis_size("patch")
    scale_inv = 1.0 / math.sqrt(coord_count)
    planes = subjects.transpose(1, 0, 2)
    partial_value = lax.dot_general(
        subjects, basis_modes, (((1, 2), (0, 1)), ((), ())), preferred_element_type=jnp.float32
    )
    reach = GHOST * laplace_blocks.shape[2]
    low, turned, after = reduce_scores(partial_value, basis_modes, reach, scale_inv)
    base, carry, scores = smoothed(basis_modes, laplace_blocks, columns, after, low)
    rate = 4.0 / (subject_count * batch)
    new_modes, norms = updated_modes(
        planes, base, carry, basis_modes, low, turned, scale_inv, rate, coord_count
    )
    return (scores, new_modes.reshape(coords, vert_count, mode_count), norms.reshape(mode_count))


def solution(mesh):
    placed = (
        P(("groups", "batch"), None, "patch"),
        P(None, ("groups", "patch"), None),
        P("patch", None, None, None),
        P("patch", None),
    )
    return jax.shard_map(
        body,
        mesh=mesh,
        in_specs=placed,
        out_specs=(P(("groups", "batch"), None), P(None, ("groups", "patch"), None), P("groups")),
        check_vma=False,
    )
```
